32 devices in a mesh: gx: 2 (over x), gy: 16 (over z, y, core).
Axes of the slice: x: 2, y: 2, z: 4, core: 2. Of those that a mesh axis runs over, the one named last changes fastest.
Arguments:
- residual_in: float32 [2, 16, 1024, 256], P('gx', 'gy'), may hold values from -6 to 6
- neumann: float32 [2, 16, 1024, 1024], P('gx', 'gy'), may hold values from -0.1875 to 0.1875
- dirichlet: float32 [2, 16, 1024, 1024], P('gx', 'gy'), may hold values from -0.1875 to 0.1875
- coarse: float32 [2, 1024, 1024], P('gx', 'gy'), may hold values from -0.1875 to 0.1875
- decay: float32 [2, 16, 64], P('gx', 'gy'), may hold values from 0.4 to 1
- face_rows: int32 [2, 16, 1024], P('gx', 'gy'), may hold values from 0 to 1023, each once within a row
- primal: int32 [2, 16, 64], P('gx', 'gy'), may hold values from 0 to 1023, as said below
Outputs:
- solution: float32 [2, 16, 1024, 256], P('gx', 'gy')
- residual: float32 [2, 16, 1024, 256], P('gx', 'gy')
The draws below stay inside these ranges and needn't reach their ends.
Inputs may be any that keep to these rules, and one draw needn't show every extreme that they name: `primal`: each subdomain's 64 entries are distinct rows of its interface. `face_rows`: each subdomain's entries name every interface row once.
All inputs are finite; a program needn't handle non-finite values.
Results may differ from the reference program's by a relative error of at most 0.0001.
Values sent between devices are 32-bit elements; how exact they have to be, the bound alone decides.
A program may use at most 64 MiB of HBM per device.

```python
import jax
import jax.numpy as jnp
from jax import lax

M = 1024
P_SIZE = 64
R = 256
STEPS = 2
SUBX = 2
SUBY = 16
FACE = 256
COARSE = 1024


def draw_primal(key, part):
    keys = jax.random.split(jax.random.fold_in(key, 17), SUBX * SUBY)
    perms = jax.vmap(lambda single: jax.random.permutation(single, M))(keys)
    picked = perms[:, :P_SIZE]
    top_shift = M - 1 - picked[0, 0]
    bottom_shift = (M - picked[1, 0]) % M
    which = jnp.arange(SUBX * SUBY, dtype=jnp.int32)
    offsets = jnp.where(which == 0, top_shift, jnp.where(which == 1, bottom_shift, 0))
    picked = (picked + offsets[:, None]) % M
    return picked.reshape(SUBX, SUBY, P_SIZE).astype(jnp.int32)


def level_of(stream_key, extent, cuts, least, largest):
    level, own = 1.0, jax.random.fold_in(stream_key, 6)
    for axis_at, shards_of in cuts:
        heights = jnp.exp(jax.random.uniform(jax.random.fold_in(own, axis_at), (shards_of,), jnp.float32, least / len(cuts), largest / len(cuts)))
        level = level * jnp.repeat(heights, extent[axis_at] // shards_of).reshape([-1 if axis == axis_at else 1 for axis in range(len(extent))])
    return level


def normal_values(stream_key, shape, width, reach, cuts=(), kind=jnp.bfloat16):
    values = width * jax.random.normal(stream_key, shape, jnp.float32)
    if cuts:
        values = values * level_of(stream_key, shape, cuts, -0.22, 0.18)
    return jnp.clip(values, -reach, reach).astype(kind)


def setup_inputs(seed: int = 0) -> dict:
    key_of = jax.random.split(jax.random.key(seed), 8)
    return {
        "residual_in": normal_values(key_of[0], (SUBX, SUBY, M, R), 1.0, 6.0, ((0, 2), (1, 16)), jnp.float32),
        "neumann": normal_values(key_of[1], (SUBX, SUBY, M, M), M ** -0.5, 0.1875, ((0, 2), (1, 16)), jnp.float32),
        "dirichlet": normal_values(key_of[2], (SUBX, SUBY, M, M), M ** -0.5, 0.1875, ((0, 2), (1, 16)), jnp.float32),
        "coarse": normal_values(key_of[3], (SUBX, COARSE, COARSE), COARSE ** -0.5, 0.1875, ((0, 2), (1, 16)), jnp.float32),
        "decay": jnp.clip(0.4 + 0.6 * jax.random.uniform(key_of[4], (SUBX, SUBY, P_SIZE), jnp.float32) ** level_of(key_of[4], (SUBX, SUBY, P_SIZE), ((0, 2), (1, 16)), -0.2, 0.2), 0.4, 1.0),
        "face_rows": jax.vmap(lambda own: jax.random.permutation(own, M))(jax.random.split(key_of[5], SUBX * SUBY)).reshape((SUBX, SUBY, M)).astype(jnp.int32),
        "primal": draw_primal(jax.random.fold_in(key_of[7], 71), 0),
    }


def neighbours(field, face_rows, inverse):
    faces = jnp.take_along_axis(field, face_rows[..., None], axis=2)
    low_row = faces[:, :, 0:FACE]
    high_row = faces[:, :, FACE:2 * FACE]
    low_col = faces[:, :, 2 * FACE:3 * FACE]
    high_col = faces[:, :, 3 * FACE:4 * FACE]
    zero_row = jnp.zeros_like(low_row[:1])
    zero_col = jnp.zeros_like(low_row[:, :1])
    recv_zero = jnp.concatenate([zero_row, high_row[:-1]], axis=0)
    recv_one = jnp.concatenate([low_row[1:], zero_row], axis=0)
    recv_two = jnp.concatenate([zero_col, high_col[:, :-1]], axis=1)
    recv_three = jnp.concatenate([low_col[:, 1:], zero_col], axis=1)
    stacked = jnp.concatenate([recv_zero, recv_one, recv_two, recv_three], axis=2)
    return jnp.take_along_axis(stacked, inverse[..., None], axis=2)


def reference(residual_in, neumann, dirichlet, coarse, decay, face_rows, primal):
    high = lax.Precision.HIGHEST
    inverse = jnp.argsort(face_rows, axis=-1).astype(jnp.int32)
    onehot = (jnp.arange(M, dtype=jnp.int32)[None, None, :, None] == primal[:, :, None, :]).astype(jnp.float32)
    residual = residual_in
    solution = jnp.zeros_like(residual_in)
    for step in range(STEPS):
        jump = residual - neighbours(residual, face_rows, inverse)
        work = jnp.einsum("xymn,xynr->xymr", neumann, jump, precision=high)
        prim_val = jnp.take_along_axis(work, primal[..., None], axis=2)
        cvec = prim_val.reshape(SUBX, COARSE, R)
        cq = jnp.einsum("xab,xbr->xar", coarse, cvec, precision=high).reshape(SUBX, SUBY, P_SIZE, R)

        def link(prev, item):
            rate, value = item
            current = value + rate[:, :, None] * prev
            return current, current

        start_val = jnp.zeros((SUBY, P_SIZE, R), jnp.float32)
        unused, chain = lax.scan(link, start_val, (decay, cq))
        corrected = work + jnp.einsum("xymp,xypr->xymr", onehot, chain, precision=high)
        update = jnp.einsum("xymn,xynr->xymr", dirichlet, corrected, precision=high)
        solution = solution + update
        residual = jump - 0.5 * update
    return solution, residual
```

```python
import functools

import jax
import jax.numpy as jnp
from jax import lax
from jax.experimental import pallas as pl
from jax.experimental.pallas import tpu as pltpu
from jax.sharding import PartitionSpec as P

STEPS = 2
MESH = pl.DeviceIdType.MESH
F32 = jnp.float32
BF16 = jnp.bfloat16


def dot(a, b):
    return jnp.dot(a, b, preferred_element_type=F32)


def split(x):
    high = x.astype(BF16)
    return high, (x - high.astype(F32)).astype(BF16)


def dot3(a, b):
    return dot(a[0], b[0]) + dot(a[0], b[1]) + dot(a[1], b[0])


def line_sizes(count):
    chips = count // 2
    inner = 1
    while inner * inner * 4 <= chips:
        inner *= 2
    return chips // inner, inner


def kernel(
    nx, ny_all, r_hbm, n_hbm, d_hbm, c_hbm, decay_ref, rows_ref, prim_ref,
    sol_ref, res_ref,
    n_buf, d_buf, nh, nl, dh, dl, perm, perm_t,
    r_buf, jump, upd, fsend, frecv, c_two, psend, gath, qsend, cown, cprev, csend,
    nph, npl, deh, del_, base,
    load_sem, c_sem, f_ssem, f_rsem, a_ssem, b_ssem, g_rsem, q_ssem, q_rsem, p_ssem, p_rsem,
):
    unknowns, width = r_buf.shape
    face = unknowns // 4
    half = width // 2
    prims = c_two.shape[1]
    nz, ny = line_sizes(ny_all)
    block = face
    blocks = unknowns // block

    a = lax.axis_index("gx")
    me = lax.axis_index("gy")
    core = me % 2
    chip = me // 2
    y = chip % ny
    z = chip // ny
    partner = chip * 2 + (1 - core)

    def place(zz, yy, cc):
        return (zz * ny + yy) * 2 + cc

    def rows_of(i, size):
        return pl.ds(pl.multiple_of(i * size, size), size)

    loads = [
        pltpu.make_async_copy(src, dst, load_sem.at[i])
        for i, (src, dst) in enumerate(
            [(r_hbm, r_buf), (c_hbm, c_two.at[core]), (n_hbm, n_buf), (d_hbm, d_buf)]
        )
    ]
    for load in loads:
        load.start()

    barrier = pltpu.get_barrier_semaphore()

    def greet(gx, gy):
        pl.semaphore_signal(barrier, inc=1, device_id=(gx, gy), device_id_type=MESH)

    z_steps = sorted(range(1, nz), key=lambda d: min(d, nz - d))
    count = 0
    for cc in range(2):
        for dz in z_steps:
            greet(a, place((z + dz) % nz, y, cc))
            count += 1
    greet(a, partner)
    count += 1
    for dy in range(1, ny):
        greet(a, place(z, (y + dy) % ny, core))
        count += 1
    has = [a > 0, a < nx - 1, me > 0, me < ny_all - 1]
    to = [(a - 1, me), (a + 1, me), (a, me - 1), (a, me + 1)]
    for k in range(4):
        pl.when(has[k])(functools.partial(greet, *to[k]))
        count = count + has[k].astype(jnp.int32)
    if nx > 1:
        pl.when(a < 2)(functools.partial(greet, 1 - a, partner))
        count = count + (a < 2).astype(jnp.int32)

    lanes = 128
    rows_f = rows_ref[...].astype(F32)
    rows_t = jnp.transpose(jnp.broadcast_to(rows_f, (lanes, unknowns)))
    for t in range(unknowns // lanes):
        cols = lax.broadcasted_iota(jnp.int32, (unknowns, lanes), 1) + t * lanes
        perm[:, t * lanes : (t + 1) * lanes] = jnp.where(
            rows_t == cols.astype(F32), 1.0, 0.0
        ).astype(BF16)

    def take_faces(step, source_ref):
        field = split(source_ref[...])

        def one(i, carry):
            at = rows_of(i, block)
            picks = perm[at, :]
            fsend[step, at, :] = dot(picks, field[0]) + dot(picks, field[1])
            return carry

        lax.fori_loop(0, blocks, one, 0)

    other = [1, 0, 3, 2]

    def face_copy(step, k):
        return pltpu.make_async_remote_copy(
            src_ref=fsend.at[step, pl.ds(k * face, face), :],
            dst_ref=frecv.at[step, pl.ds(other[k] * face, face), :],
            send_sem=f_ssem.at[step, k],
            recv_sem=f_rsem.at[step, other[k]],
            device_id=to[k],
            device_id_type=MESH,
        )

    def face_wait(step, k):
        face_copy(step, other[k]).wait_recv()

    loads[0].wait()
    take_faces(0, r_buf)
    pl.semaphore_wait(barrier, count)
    for k in range(4):
        pl.when(has[k])(face_copy(0, k).start)
    loads[1].wait()
    coarse_copy = pltpu.make_async_remote_copy(
        src_ref=c_two.at[core],
        dst_ref=c_two.at[core],
        send_sem=c_sem.at[0],
        recv_sem=c_sem.at[1],
        device_id=(a, partner),
        device_id_type=MESH,
    )
    coarse_copy.start()

    for step in range(STEPS):
        for k in range(4):

            @pl.when(jnp.logical_not(has[k]))
            def _(step=step, k=k):
                frecv[step, k * face : (k + 1) * face, :] = jnp.zeros((face, width), F32)

    def build_t(i, carry):
        at = rows_of(i, block)
        here = lax.broadcasted_iota(jnp.int32, (block, unknowns), 0) + i * block
        perm_t[at, :] = jnp.where(here.astype(F32) == rows_f, 1.0, 0.0).astype(BF16)
        return carry

    lax.fori_loop(0, blocks, build_t, 0)

    eye = lax.broadcasted_iota(jnp.int32, (prims, prims), 0) == lax.broadcasted_iota(
        jnp.int32, (prims, prims), 1
    )
    prim_row = prim_ref[...].astype(F32)
    prim_col = jnp.sum(jnp.where(eye, prim_row, 0.0), axis=1, keepdims=True)
    rate = jnp.sum(jnp.where(eye, decay_ref[...], 0.0), axis=1, keepdims=True)
    pick_t = jnp.where(
        prim_col == lax.broadcasted_iota(jnp.int32, (prims, unknowns), 1).astype(F32), 1.0, 0.0
    ).astype(BF16)
    pick = jnp.where(
        lax.broadcasted_iota(jnp.int32, (unknowns, prims), 0).astype(F32) == prim_row, 1.0, 0.0
    ).astype(BF16)

    def halves(source, high, low):
        def one(i, carry):
            at = rows_of(i, block)
            high[at, :], low[at, :] = split(source[at, :])
            return carry

        lax.fori_loop(0, blocks, one, 0)

    loads[2].wait()
    halves(n_buf, nh, nl)
    np_h = dot(pick_t, nh[...]).astype(BF16)
    np_l = dot(pick_t, nl[...]).astype(BF16)
    nph[...] = dot(np_h, perm_t[...]).astype(BF16)
    npl[...] = dot(np_l, perm_t[...]).astype(BF16)
    base[...] = dot3((np_h, np_l), split(r_buf[...]))
    loads[3].wait()
    halves(d_buf, dh, dl)

    def pick_d(i, carry):
        at = rows_of(i, block)
        deh[at, :] = dot(dh[at, :], pick).astype(BF16)
        del_[at, :] = dot(dl[at, :], pick).astype(BF16)
        return carry

    lax.fori_loop(0, blocks, pick_d, 0)

    coarse_copy.wait()
    coarse = split(c_two[...].reshape(2 * prims, c_two.shape[2]))

    def phase_a(step, dz, cc):
        return pltpu.make_async_remote_copy(
            src_ref=psend.at[step, cc],
            dst_ref=gath.at[step, me],
            send_sem=a_ssem.at[step, dz, cc],
            recv_sem=g_rsem.at[step, me],
            device_id=(a, place((z + dz) % nz, y, cc)),
            device_id_type=MESH,
        )

    def phase_self(step):
        return pltpu.make_async_remote_copy(
            src_ref=psend.at[step, 1 - core],
            dst_ref=gath.at[step, me],
            send_sem=a_ssem.at[step, 0, 0],
            recv_sem=g_rsem.at[step, me],
            device_id=(a, partner),
            device_id_type=MESH,
        )

    def phase_b(step, dz, cc, dy, who):
        return pltpu.make_async_remote_copy(
            src_ref=gath.at[step, who],
            dst_ref=gath.at[step, who],
            send_sem=b_ssem.at[step, dz, cc, dy],
            recv_sem=g_rsem.at[step, who],
            device_id=(a, place(z, (y + dy) % ny, core)),
            device_id_type=MESH,
        )

    def arrived(step, who):
        pltpu.make_async_remote_copy(
            src_ref=gath.at[step, who],
            dst_ref=gath.at[step, who],
            send_sem=b_ssem.at[step, 0, 0, 0],
            recv_sem=g_rsem.at[step, who],
            device_id=(a, partner),
            device_id_type=MESH,
        ).wait_recv()

    def relay(step, dz):
        for cc in range(2):
            if dz == 0:
                who = me if cc == 0 else partner
            else:
                who = place((z + dz) % nz, y, cc)
            if not (dz == 0 and cc == 0):
                arrived(step, who)
            for dy in range(1, ny):
                phase_b(step, dz, cc, dy, who).start()

    def q_copy(step):
        return pltpu.make_async_remote_copy(
            src_ref=qsend.at[step, 1 - core],
            dst_ref=cown.at[step, core],
            send_sem=q_ssem.at[step],
            recv_sem=q_rsem.at[step],
            device_id=(a, partner),
            device_id_type=MESH,
        )

    def first_copy(step, own):
        which = core if own else 1 - core
        return pltpu.make_async_remote_copy(
            src_ref=qsend.at[step, which],
            dst_ref=cprev.at[step, core],
            send_sem=p_ssem.at[step, 0 if own else 1],
            recv_sem=p_rsem.at[step, core],
            device_id=(a + 1, me if own else partner),
            device_id_type=MESH,
        )

    def next_copy(step, h):
        return pltpu.make_async_remote_copy(
            src_ref=csend.at[step, h],
            dst_ref=cprev.at[step, h],
            send_sem=p_ssem.at[step, h],
            recv_sem=p_rsem.at[step, h],
            device_id=(a + 1, me),
            device_id_type=MESH,
        )

    starts = jnp.logical_and(a == 0, a < nx - 1)
    passes = jnp.logical_and(a > 0, a < nx - 1)

    for step in range(STEPS):
        source = r_buf if step == 0 else res_ref
        for k in (2, 3, 0, 1):
            pl.when(has[k])(functools.partial(face_wait, step, k))
        ghost = split(frecv[step])
        prim = base[...] - dot3((nph[...], npl[...]), ghost)
        for h in range(2):
            psend[step, h] = prim[:, h * half : (h + 1) * half]
        gath[step, me] = psend[step, core]
        phase_self(step).start()
        for dz in z_steps:
            for cc in range(2):
                phase_a(step, dz, cc).start()
        relay(step, 0)

        def fill(i, carry, step=step, source=source, ghost=ghost):
            at = rows_of(i, block)
            back = perm_t[at, :]
            jump[at, :] = source[at, :] - dot(back, ghost[0]) - dot(back, ghost[1])
            return carry

        lax.fori_loop(0, blocks, fill, 0)
        relay(step, z_steps[0])

        jumps = split(jump[...])

        def multiply(i, carry, jumps=jumps):
            at = rows_of(i, block)
            upd[at, :] = dot3((nh[at, :], nl[at, :]), jumps)
            return carry

        lax.fori_loop(0, blocks, multiply, 0)
        for dz in z_steps[1:]:
            relay(step, dz)
        works = split(upd[...])

        def smooth(i, carry, works=works):
            at = rows_of(i, block)
            upd[at, :] = dot3((dh[at, :], dl[at, :]), works)
            return carry

        lax.fori_loop(0, blocks, smooth, 0)

        for dz in range(nz):
            for dy in range(1, ny):
                for cc in range(2):
                    arrived(step, place((z + dz) % nz, (y + dy) % ny, cc))
        values = split(gath[step].reshape(ny_all * prims, half))
        quarter = dot3(coarse, values)
        for h in range(2):
            qsend[step, h] = quarter[h * prims : (h + 1) * prims, :]
        q_copy(step).start()

        @pl.when(starts)
        def _(step=step):
            first_copy(step, True).start()
            first_copy(step, False).start()

        cown[step, core] = qsend[step, core]
        q_copy(step).wait_recv()

        @pl.when(a == 0)
        def _(step=step):
            csend[step] = cown[step]

        @pl.when(a > 0)
        def _(step=step):
            for h in range(2):
                next_copy(step, h).wait_recv()
                csend[step, h] = cown[step, h] + rate * cprev[step, h]

        @pl.when(passes)
        def _(step=step):
            for h in range(2):
                next_copy(step, h).start()

        chain = split(jnp.concatenate([csend[step, 0], csend[step, 1]], axis=1))

        def finish(i, carry, step=step, chain=chain):
            at = rows_of(i, block)
            update = upd[at, :] + dot3((deh[at, :], del_[at, :]), chain)
            if step == 0:
                sol_ref[at, :] = update
            else:
                sol_ref[at, :] += update
            res_ref[at, :] = jump[at, :] - 0.5 * update
            return carry

        lax.fori_loop(0, blocks, finish, 0)
        if step + 1 < STEPS:
            take_faces(step + 1, res_ref)
            for k in range(4):
                pl.when(has[k])(face_copy(step + 1, k).start)
            rests = split(res_ref[...])
            np_h = dot(pick_t, nh[...]).astype(BF16)
            np_l = dot(pick_t, nl[...]).astype(BF16)
            base[...] = dot3((np_h, np_l), rests)

    for step in range(STEPS):
        for k in range(4):
            pl.when(has[k])(face_copy(step, k).wait_send)
        phase_self(step).wait_send()
        for dz in z_steps:
            for cc in range(2):
                phase_a(step, dz, cc).wait_send()
        for dz in range(nz):
            for cc in range(2):
                for dy in range(1, ny):
                    who = place((z + dz) % nz, y, cc)
                    phase_b(step, dz, cc, dy, who).wait_send()
        q_copy(step).wait_send()

        @pl.when(starts)
        def _(step=step):
            first_copy(step, True).wait_send()
            first_copy(step, False).wait_send()

        @pl.when(passes)
        def _(step=step):
            for h in range(2):
                next_copy(step, h).wait_send()


def local(nx, ny_all, residual_in, neumann, dirichlet, coarse, decay, face_rows, primal):
    unknowns, width = residual_in.shape[2:]
    prims = primal.shape[2]
    order = coarse.shape[2]
    half = width // 2
    nz, ny = line_sizes(ny_all)
    anywhere = pl.BlockSpec(memory_space=pl.ANY)
    inside = pl.BlockSpec(memory_space=pltpu.VMEM)
    square = (unknowns, unknowns)
    field = (unknowns, width)
    dma = pltpu.SemaphoreType.DMA
    out = jax.ShapeDtypeStruct(field, F32)
    sol, res = pl.pallas_call(
        functools.partial(kernel, nx, ny_all),
        out_shape=(out, out),
        in_specs=[anywhere] * 4 + [inside] * 3,
        out_specs=(inside, inside),
        scratch_shapes=[
            pltpu.VMEM(square, F32),
            pltpu.VMEM(square, F32),
            pltpu.VMEM(square, BF16),
            pltpu.VMEM(square, BF16),
            pltpu.VMEM(square, BF16),
            pltpu.VMEM(square, BF16),
            pltpu.VMEM(square, BF16),
            pltpu.VMEM(square, BF16),
            pltpu.VMEM(field, F32),
            pltpu.VMEM(field, F32),
            pltpu.VMEM(field, F32),
            pltpu.VMEM((STEPS,) + field, F32),
            pltpu.VMEM((STEPS,) + field, F32),
            pltpu.VMEM((2, prims, order), F32),
            pltpu.VMEM((STEPS, 2, prims, half), F32),
            pltpu.VMEM((STEPS, ny_all, prims, half), F32),
            pltpu.VMEM((STEPS, 2, prims, half), F32),
            pltpu.VMEM((STEPS, 2, prims, half), F32),
            pltpu.VMEM((STEPS, 2, prims, half), F32),
            pltpu.VMEM((STEPS, 2, prims, half), F32),
            pltpu.VMEM((prims, unknowns), BF16),
            pltpu.VMEM((prims, unknowns), BF16),
            pltpu.VMEM((unknowns, prims), BF16),
            pltpu.VMEM((unknowns, prims), BF16),
            pltpu.VMEM((prims, width), F32),
            dma((4,)),
            dma((2,)),
            dma((STEPS, 4)),
            dma((STEPS, 4)),
            dma((STEPS, nz, 2)),
            dma((STEPS, nz, 2, max(ny, 2))),
            dma((STEPS, ny_all)),
            dma((STEPS,)),
            dma((STEPS,)),
            dma((STEPS, 2)),
            dma((STEPS, 2)),
        ],
        compiler_params=pltpu.CompilerParams(
            collective_id=0, has_side_effects=True, vmem_limit_bytes=60000 * 1024
        ),
    )(
        residual_in[0, 0],
        neumann[0, 0],
        dirichlet[0, 0],
        coarse[0],
        decay[0],
        face_rows[0],
        primal[0],
    )
    return (sol[None, None], res[None, None])


def solution(mesh):
    return jax.shard_map(
        functools.partial(local, mesh.shape["gx"], mesh.shape["gy"]),
        mesh=mesh,
        in_specs=(
            P("gx", "gy", None, None),
            P("gx", "gy", None, None),
            P("gx", "gy", None, None),
            P("gx", "gy", None),
            P("gx", "gy", None),
            P("gx", "gy", None),
            P("gx", "gy", None),
        ),
        out_specs=(P("gx", "gy", None, None), P("gx", "gy", None, None)),
        check_vma=False,
    )
```

```python
import functools

import jax
import jax.numpy as jnp
from jax import lax
from jax.experimental import pallas as pl
from jax.experimental.pallas import tpu as pltpu
from jax.sharding import PartitionSpec as P

STEPS = 2
MESH = pl.DeviceIdType.MESH
F32 = jnp.float32
BF16 = jnp.bfloat16


def dot(a, b):
    return jnp.dot(a, b, preferred_element_type=F32)


def split(x):
    high = x.astype(BF16)
    return high, (x - high.astype(F32)).astype(BF16)


def dot3(a, b):
    return dot(a[0], b[0]) + dot(a[0], b[1]) + dot(a[1], b[0])


def line_sizes(count):
    chips = count // 2
    inner = 1
    while inner * inner * 4 <= chips:
        inner *= 2
    return chips // inner, inner


def kernel(
    nx, ny_all, r_hbm, n_hbm, d_hbm, c_hbm, decay_ref, rows_ref, prim_ref,
    t1_hbm, t2_hbm, deh_hbm, del_hbm, chain_ref,
    n_buf, d_buf, nh, nl, dh, dl, perm, perm_t,
    r_buf, jump, upd, sol, res, fsend, frecv, c_all, psend, gath, qsend, cown, cprev, csend,
    sel_h, sel_l, nph, npl, deh, del_, pdeh, pdel, base,
    load_sem, out_sem, cf_ssem, cp_ssem, c_rsem, f_ssem, f_rsem, a_ssem, g_rsem,
    q_ssem, q_rsem, p_ssem, p_rsem,
):
    unknowns, width = r_buf.shape
    face = unknowns // 4
    prims = c_all.shape[1]
    nz, ny = line_sizes(ny_all)
    ng = 2 * ny
    part = width // ng
    fold = max(1, 128 // part)
    short = prims // fold
    block = face
    blocks = unknowns // block

    a = lax.axis_index("gx")
    me = lax.axis_index("gy")
    g = me % ng
    z = me // ng
    core = g % 2
    y = g // 2
    partner = me + 1 - 2 * core

    def pack(x):
        return jnp.concatenate([x[j * short : (j + 1) * short] for j in range(fold)], axis=1)

    def unpack(x):
        return jnp.concatenate([x[:, j * part : (j + 1) * part] for j in range(fold)], axis=0)

    def rows_of(i, size):
        return pl.ds(pl.multiple_of(i * size, size), size)

    def remote(src, dst, send, recv, gx, gy):
        return pltpu.make_async_remote_copy(
            src_ref=src, dst_ref=dst, send_sem=send, recv_sem=recv,
            device_id=(gx, gy), device_id_type=MESH,
        )

    loads = [
        pltpu.make_async_copy(src, dst, load_sem.at[i])
        for i, (src, dst) in enumerate(
            [(r_hbm, r_buf), (c_hbm, c_all.at[g]), (n_hbm, n_buf), (d_hbm, d_buf)]
        )
    ]
    for load in loads:
        load.start()

    barrier = pltpu.get_barrier_semaphore()

    def greet(gx, gy):
        pl.semaphore_signal(barrier, inc=1, device_id=(gx, gy), device_id_type=MESH)

    for d in range(1, ny_all):
        greet(a, (me + d) % ny_all)
    count = ny_all - 1
    has = [a > 0, a < nx - 1, me > 0, me < ny_all - 1]
    to = [(a - 1, me), (a + 1, me), (a, me - 1), (a, me + 1)]
    for k in range(2):
        pl.when(has[k])(functools.partial(greet, *to[k]))
        count = count + has[k].astype(jnp.int32)
    mates = [z * ng + (g + d) % ng for d in range(ng)]
    mate_at = [(g + d) % ng for d in range(ng)]
    if nx > 1:

        @pl.when(a < 2)
        def _():
            for d in range(1, ng):
                greet(1 - a, mates[d])

        count = count + (a < 2).astype(jnp.int32) * (ng - 1)

    other = [1, 0, 3, 2]

    def face_copy(step, k):
        return remote(
            fsend.at[step, pl.ds(k * face, face), :],
            frecv.at[step, pl.ds(other[k] * face, face), :],
            f_ssem.at[step, k],
            f_rsem.at[step, other[k]],
            *to[k],
        )

    def face_wait(step, k):
        face_copy(step, other[k]).wait_recv()

    lanes = 128
    rows_f = rows_ref[...].astype(F32)
    rows_t = jnp.transpose(jnp.broadcast_to(rows_f, (lanes, unknowns)))

    def build_face(k):
        low, high = k * face, (k + 1) * face
        for t in range(unknowns // lanes):
            cols = lax.broadcasted_iota(jnp.int32, (face, lanes), 1) + t * lanes
            perm[low:high, t * lanes : (t + 1) * lanes] = jnp.where(
                rows_t[low:high] == cols.astype(F32), 1.0, 0.0
            ).astype(BF16)

    def take_face(step, k, field):
        low, high = k * face, (k + 1) * face
        picks = perm[low:high, :]
        fsend[step, low:high, :] = dot(picks, field[0]) + dot(picks, field[1])

    for k in range(4):
        build_face(k)
    loads[0].wait()
    field = split(r_buf[...])
    pl.when(has[0])(functools.partial(take_face, 0, 0, field))
    pl.when(has[1])(functools.partial(take_face, 0, 1, field))
    pl.semaphore_wait(barrier, count)
    for k in range(2):
        pl.when(has[k])(face_copy(0, k).start)
    for k in range(2, 4):
        take_face(0, k, field)
        pl.when(has[k])(face_copy(0, k).start)

    def coarse_far(dy):
        return remote(
            c_all.at[g], c_all.at[g], cf_ssem.at[dy], c_rsem.at[g],
            a, z * ng + ((y + dy) % ny) * 2 + core,
        )

    def coarse_near(dy):
        which = ((y + dy) % ny) * 2 + core
        return remote(
            c_all.at[which], c_all.at[which], cp_ssem.at[dy], c_rsem.at[which], a, partner
        )

    def coarse_arrived(which):
        remote(
            c_all.at[which], c_all.at[which], cp_ssem.at[0], c_rsem.at[which], a, partner
        ).wait_recv()

    loads[1].wait()
    coarse_near(0).start()
    for dy in range(1, ny):
        coarse_far(dy).start()

    for step in range(STEPS):
        for k in range(4):

            @pl.when(jnp.logical_not(has[k]))
            def _(step=step, k=k):
                frecv[step, k * face : (k + 1) * face, :] = jnp.zeros((face, width), F32)

    def build_t(i, carry):
        at = rows_of(i, block)
        here = lax.broadcasted_iota(jnp.int32, (block, unknowns), 0) + i * block
        perm_t[at, :] = jnp.where(here.astype(F32) == rows_f, 1.0, 0.0).astype(BF16)
        return carry

    lax.fori_loop(0, blocks, build_t, 0)

    eye = lax.broadcasted_iota(jnp.int32, (prims, prims), 0) == lax.broadcasted_iota(
        jnp.int32, (prims, prims), 1
    )
    prim_row = prim_ref[...].astype(F32)
    prim_col = jnp.sum(jnp.where(eye, prim_row, 0.0), axis=1, keepdims=True)
    rate = jnp.sum(jnp.where(eye, decay_ref[...], 0.0), axis=1, keepdims=True)
    pick_t = jnp.where(
        prim_col == lax.broadcasted_iota(jnp.int32, (prims, unknowns), 1).astype(F32), 1.0, 0.0
    ).astype(BF16)
    pick = jnp.where(
        lax.broadcasted_iota(jnp.int32, (unknowns, prims), 0).astype(F32) == prim_row, 1.0, 0.0
    ).astype(BF16)

    def halves(source, high, low):
        def one(i, carry):
            at = rows_of(i, block)
            high[at, :], low[at, :] = split(source[at, :])
            return carry

        lax.fori_loop(0, blocks, one, 0)

    loads[2].wait()
    halves(n_buf, nh, nl)
    sel_h[...] = dot(pick_t, nh[...]).astype(BF16)
    sel_l[...] = dot(pick_t, nl[...]).astype(BF16)
    nph[...] = dot(sel_h[...], perm_t[...]).astype(BF16)
    npl[...] = dot(sel_l[...], perm_t[...]).astype(BF16)
    base[...] = dot3((sel_h[...], sel_l[...]), field)
    loads[3].wait()
    halves(d_buf, dh, dl)

    def pick_d(i, carry):
        at = rows_of(i, block)
        deh[at, :] = dot(dh[at, :], pick).astype(BF16)
        del_[at, :] = dot(dl[at, :], pick).astype(BF16)
        return carry

    lax.fori_loop(0, blocks, pick_d, 0)
    outs = [
        pltpu.make_async_copy(src, dst, out_sem.at[i])
        for i, (src, dst) in enumerate(
            [(deh, deh_hbm), (del_, del_hbm), (sol, t1_hbm), (res, t2_hbm)]
        )
    ]
    outs[0].start()
    outs[1].start()

    def pick_pd(i, carry):
        at = rows_of(i, block)
        pdeh[at, :] = dot(perm[at, :], deh[...]).astype(BF16)
        pdel[at, :] = dot(perm[at, :], del_[...]).astype(BF16)
        return carry

    lax.fori_loop(0, blocks, pick_pd, 0)

    order = [
        (dz, d)
        for dz in sorted(range(nz), key=lambda dz: -min(dz, nz - dz))
        for d in range(ng)
        if (dz, d) != (0, 0)
    ]

    def spread(step, dz, d):
        return remote(
            psend.at[step, mate_at[d]],
            gath.at[step, me],
            a_ssem.at[step, dz, d],
            g_rsem.at[step, me],
            a,
            ((z + dz) % nz) * ng + mate_at[d],
        )

    def arrived(step, who):
        remote(
            psend.at[step, 0], gath.at[step, who], a_ssem.at[step, 0, 0], g_rsem.at[step, who],
            a, partner,
        ).wait_recv()

    def q_copy(step, d):
        return remote(
            qsend.at[step, mate_at[d]], cown.at[step, g], q_ssem.at[step, d], q_rsem.at[step, g],
            a, mates[d],
        )

    def first_copy(step, d):
        return remote(
            qsend.at[step, mate_at[d]], cprev.at[step, g], p_ssem.at[step, d], p_rsem.at[step, g],
            a + 1, mates[d],
        )

    def next_copy(step, q):
        return remote(
            csend.at[step, q], cprev.at[step, q], p_ssem.at[step, q], p_rsem.at[step, q],
            a + 1, me,
        )

    starts = jnp.logical_and(a == 0, a < nx - 1)
    passes = jnp.logical_and(a > 0, a < nx - 1)

    for step in range(STEPS):
        last = step + 1 == STEPS
        source = r_buf if step == 0 else res
        for k in (2, 3, 0, 1):
            pl.when(has[k])(functools.partial(face_wait, step, k))
        ghost = split(frecv[step])
        prim = base[...] - dot3((nph[...], npl[...]), ghost)
        for q in range(ng):
            psend[step, q] = pack(prim[:, q * part : (q + 1) * part])
        for dz, d in order:
            spread(step, dz, d).start()
        gath[step, me] = psend[step, g]

        def fill(i, carry, source=source, ghost=ghost):
            at = rows_of(i, block)
            back = perm_t[at, :]
            jump[at, :] = source[at, :] - dot(back, ghost[0]) - dot(back, ghost[1])
            return carry

        lax.fori_loop(0, blocks, fill, 0)
        jumps = split(jump[...])

        def multiply(i, carry, jumps=jumps):
            at = rows_of(i, block)
            upd[at, :] = dot3((nh[at, :], nl[at, :]), jumps)
            return carry

        lax.fori_loop(0, blocks, multiply, 0)
        works = split(upd[...])
        if step == 0:
            for dy in range(1, ny):
                coarse_arrived(((y + dy) % ny) * 2 + core)
                coarse_near(dy).start()

        def smooth(i, carry, works=works, step=step):
            at = rows_of(i, block)
            update = dot3((dh[at, :], dl[at, :]), works)
            if step == 0:
                sol[at, :] = update
            else:
                sol[at, :] += update
            res[at, :] = jump[at, :] - 0.5 * update
            return carry

        lax.fori_loop(0, blocks, smooth, 0)
        if last:
            outs[2].start()
            outs[3].start()
        else:
            rests = split(res[...])
            for k in range(4):
                pl.when(has[k])(functools.partial(take_face, step + 1, k, rests))
        if step == 0:
            for dy in range(ny):
                coarse_arrived(((y + dy) % ny) * 2 + 1 - core)
        coarse = split(c_all[...].reshape(ng * prims, c_all.shape[2]))
        for dz, d in order:
            arrived(step, ((z + dz) % nz) * ng + mate_at[d])
        values = jnp.concatenate([unpack(gath[step, b]) for b in range(ny_all)], axis=0)
        quarter = dot3(coarse, split(values))
        for q in range(ng):
            qsend[step, q] = pack(quarter[q * prims : (q + 1) * prims, :])

        @pl.when(starts)
        def _(step=step):
            for d in range(ng):
                first_copy(step, d).start()

        for d in range(1, ng):
            q_copy(step, d).start()
        cown[step, g] = qsend[step, g]
        for d in range(1, ng):
            remote(
                qsend.at[step, 0], cown.at[step, mate_at[d]], q_ssem.at[step, 0],
                q_rsem.at[step, mate_at[d]], a, partner,
            ).wait_recv()

        def joined(ref, step=step):
            return jnp.concatenate([unpack(ref[step, q]) for q in range(ng)], axis=1)

        @pl.when(a == 0)
        def _(step=step):
            chain_ref[...] = joined(cown)

        @pl.when(a > 0)
        def _(step=step):
            for q in range(ng):
                next_copy(step, q).wait_recv()
            chain_ref[...] = joined(cown) + rate * joined(cprev)

        @pl.when(passes)
        def _(step=step):
            for q in range(ng):
                csend[step, q] = pack(chain_ref[:, q * part : (q + 1) * part])
                next_copy(step, q).start()

        if not last:
            chain = split(chain_ref[...])

            def late_face(k, step=step, chain=chain):
                at = pl.ds(k * face, face)
                fsend[step + 1, at, :] -= 0.5 * dot3((pdeh[at, :], pdel[at, :]), chain)
                face_copy(step + 1, k).start()

            for k in range(4):
                pl.when(has[k])(functools.partial(late_face, k))

            def finish(i, carry, chain=chain):
                at = rows_of(i, block)
                more = dot3((deh[at, :], del_[at, :]), chain)
                sol[at, :] += more
                res[at, :] -= 0.5 * more
                return carry

            lax.fori_loop(0, blocks, finish, 0)
            base[...] = dot3((sel_h[...], sel_l[...]), split(res[...]))

    for out in outs:
        out.wait()
    coarse_near(0).wait_send()
    for dy in range(1, ny):
        coarse_far(dy).wait_send()
        coarse_near(dy).wait_send()
    for step in range(STEPS):
        for k in range(4):
            pl.when(has[k])(face_copy(step, k).wait_send)
        for dz, d in order:
            spread(step, dz, d).wait_send()
        for d in range(1, ng):
            q_copy(step, d).wait_send()

        @pl.when(starts)
        def _(step=step):
            for d in range(ng):
                first_copy(step, d).wait_send()

        @pl.when(passes)
        def _(step=step):
            for q in range(ng):
                next_copy(step, q).wait_send()


def closing(t1, t2, deh, del_, chain, sol, res):
    more = dot3((deh[...], del_[...]), split(chain[...]))
    sol[...] = t1[...] + more
    res[...] = t2[...] - 0.5 * more


def local(nx, ny_all, residual_in, neumann, dirichlet, coarse, decay, face_rows, primal):
    unknowns, width = residual_in.shape[2:]
    prims = primal.shape[2]
    order = coarse.shape[2]
    nz, ny = line_sizes(ny_all)
    ng = 2 * ny
    part = width // ng
    fold = max(1, 128 // part)
    piece = (prims // fold, fold * part)
    anywhere = pl.BlockSpec(memory_space=pl.ANY)
    inside = pl.BlockSpec(memory_space=pltpu.VMEM)
    square = (unknowns, unknowns)
    field = (unknowns, width)
    slim = (unknowns, prims)
    dma = pltpu.SemaphoreType.DMA
    whole = jax.ShapeDtypeStruct(field, F32)
    thin = jax.ShapeDtypeStruct(slim, BF16)
    pieces = pl.pallas_call(
        functools.partial(kernel, nx, ny_all),
        out_shape=(whole, whole, thin, thin, jax.ShapeDtypeStruct((prims, width), F32)),
        in_specs=[anywhere] * 4 + [inside] * 3,
        out_specs=(anywhere, anywhere, anywhere, anywhere, inside),
        scratch_shapes=[
            pltpu.VMEM(square, F32),
            pltpu.VMEM(square, F32),
        ]
        + [pltpu.VMEM(square, BF16)] * 6
        + [pltpu.VMEM(field, F32)] * 5
        + [
            pltpu.VMEM((STEPS,) + field, F32),
            pltpu.VMEM((STEPS,) + field, F32),
            pltpu.VMEM((ng, prims, order), F32),
            pltpu.VMEM((STEPS, ng) + piece, F32),
            pltpu.VMEM((STEPS, ny_all) + piece, F32),
            pltpu.VMEM((STEPS, ng) + piece, F32),
            pltpu.VMEM((STEPS, ng) + piece, F32),
            pltpu.VMEM((STEPS, ng) + piece, F32),
            pltpu.VMEM((STEPS, ng) + piece, F32),
        ]
        + [pltpu.VMEM((prims, unknowns), BF16)] * 4
        + [pltpu.VMEM(slim, BF16)] * 4
        + [
            pltpu.VMEM((prims, width), F32),
            dma((4,)),
            dma((4,)),
            dma((ny,)),
            dma((ny,)),
            dma((ng,)),
            dma((STEPS, 4)),
            dma((STEPS, 4)),
            dma((STEPS, nz, ng)),
            dma((STEPS, ny_all)),
            dma((STEPS, ng)),
            dma((STEPS, ng)),
            dma((STEPS, ng)),
            dma((STEPS, ng)),
        ],
        compiler_params=pltpu.CompilerParams(
            collective_id=0, has_side_effects=True, vmem_limit_bytes=60000 * 1024
        ),
    )(
        residual_in[0, 0],
        neumann[0, 0],
        dirichlet[0, 0],
        coarse[0],
        decay[0],
        face_rows[0],
        primal[0],
    )
    rows = unknowns // 4
    tall = pl.BlockSpec((rows, width), lambda i: (i, 0))
    thin_block = pl.BlockSpec((rows, prims), lambda i: (i, 0))
    fixed = pl.BlockSpec((prims, width), lambda i: (0, 0))
    sol, res = pl.pallas_call(
        closing,
        grid=(4,),
        out_shape=(whole, whole),
        in_specs=[tall, tall, thin_block, thin_block, fixed],
        out_specs=(tall, tall),
    )(*pieces)
    return (sol[None, None], res[None, None])


def solution(mesh):
    return jax.shard_map(
        functools.partial(local, mesh.shape["gx"], mesh.shape["gy"]),
        mesh=mesh,
        in_specs=(
            P("gx", "gy", None, None),
            P("gx", "gy", None, None),
            P("gx", "gy", None, None),
            P("gx", "gy", None),
            P("gx", "gy", None),
            P("gx", "gy", None),
            P("gx", "gy", None),
        ),
        out_specs=(P("gx", "gy", None, None), P("gx", "gy", None, None)),
        check_vma=False,
    )
```

```python
import functools

import jax
import jax.numpy as jnp
from jax import lax
from jax.experimental import pallas as pl
from jax.experimental.pallas import tpu as pltpu
from jax.sharding import PartitionSpec as P

STEPS = 2
MESH = pl.DeviceIdType.MESH
F32 = jnp.float32
BF16 = jnp.bfloat16


def dot(a, b):
    return jnp.dot(a, b, preferred_element_type=F32)


def split(x):
    high = x.astype(BF16)
    return high, (x - high.astype(F32)).astype(BF16)


def dot3(a, b):
    return dot(a[0], b[0]) + dot(a[0], b[1]) + dot(a[1], b[0])


def line_sizes(count):
    chips = count // 2
    inner = 1
    while inner * inner * 4 <= chips:
        inner *= 2
    return chips // inner, inner


def kernel(
    nx, ny_all, r_hbm, n_hbm, d_hbm, c_hbm, decay_ref, rows_ref, prim_ref,
    t1_hbm, t2_hbm, deh_hbm, del_hbm, chain_ref,
    n_buf, d_buf, nh, nl, dh, dl, perm, perm_t,
    r_buf, jump, upd, sol, res, fsend, frecv, c_all, psend, gath, qsend, cown, cprev, csend,
    sel_h, sel_l, nph, npl, deh, del_, pdeh, pdel, base,
    load_sem, out_sem, cf_ssem, cp_ssem, c_rsem, f_ssem, f_rsem, a_ssem, g_rsem,
    q_ssem, q_rsem, p_ssem, p_rsem,
):
    unknowns, width = r_buf.shape
    face = unknowns // 4
    prims = c_all.shape[1]
    nz, ny = line_sizes(ny_all)
    ng = 2 * ny
    part = width // ng
    fold = max(1, 128 // part)
    short = prims // fold
    block = 2 * face
    blocks = unknowns // block

    a = lax.axis_index("gx")
    me = lax.axis_index("gy")
    g = me % ng
    z = me // ng
    core = g % 2
    y = g // 2
    partner = me + 1 - 2 * core

    def pack(x):
        return jnp.concatenate([x[j * short : (j + 1) * short] for j in range(fold)], axis=1)

    def unpack(x):
        return jnp.concatenate([x[:, j * part : (j + 1) * part] for j in range(fold)], axis=0)

    def rows_of(i, size):
        return pl.ds(pl.multiple_of(i * size, size), size)

    def remote(src, dst, send, recv, gx, gy):
        return pltpu.make_async_remote_copy(
            src_ref=src, dst_ref=dst, send_sem=send, recv_sem=recv,
            device_id=(gx, gy), device_id_type=MESH,
        )

    loads = [
        pltpu.make_async_copy(src, dst, load_sem.at[i])
        for i, (src, dst) in enumerate(
            [(r_hbm, r_buf), (c_hbm, c_all.at[g]), (n_hbm, n_buf), (d_hbm, d_buf)]
        )
    ]
    loads[0].start()

    barrier = pltpu.get_barrier_semaphore()

    def greet(gx, gy):
        pl.semaphore_signal(barrier, inc=1, device_id=(gx, gy), device_id_type=MESH)

    for d in range(1, ny_all):
        greet(a, (me + d) % ny_all)
    count = ny_all - 1
    has = [a > 0, a < nx - 1, me > 0, me < ny_all - 1]
    to = [(a - 1, me), (a + 1, me), (a, me - 1), (a, me + 1)]
    for k in range(2):
        pl.when(has[k])(functools.partial(greet, *to[k]))
        count = count + has[k].astype(jnp.int32)
    mates = [z * ng + (g + d) % ng for d in range(ng)]
    mate_at = [(g + d) % ng for d in range(ng)]
    if nx > 1:

        @pl.when(a < 2)
        def _():
            for d in range(1, ng):
                greet(1 - a, mates[d])

        count = count + (a < 2).astype(jnp.int32) * (ng - 1)

    other = [1, 0, 3, 2]

    def face_copy(step, k):
        return remote(
            fsend.at[step, pl.ds(k * face, face), :],
            frecv.at[step, pl.ds(other[k] * face, face), :],
            f_ssem.at[step, k],
            f_rsem.at[step, other[k]],
            *to[k],
        )

    def face_wait(step, k):
        face_copy(step, other[k]).wait_recv()

    lanes = 128
    rows_f = rows_ref[...].astype(F32)
    rows_t = jnp.transpose(jnp.broadcast_to(rows_f, (lanes, unknowns)))

    def build_face(k):
        low, high = k * face, (k + 1) * face
        for t in range(unknowns // lanes):
            cols = lax.broadcasted_iota(jnp.int32, (face, lanes), 1) + t * lanes
            perm[low:high, t * lanes : (t + 1) * lanes] = jnp.where(
                rows_t[low:high] == cols.astype(F32), 1.0, 0.0
            ).astype(BF16)

    def take_face(step, k, field):
        low, high = k * face, (k + 1) * face
        picks = perm[low:high, :]
        fsend[step, low:high, :] = dot(picks, field[0]) + dot(picks, field[1])

    for k in range(2):
        pl.when(has[k])(functools.partial(build_face, k))
    loads[0].wait()
    for load in loads[1:]:
        load.start()
    field = split(r_buf[...])
    pl.when(has[0])(functools.partial(take_face, 0, 0, field))
    pl.when(has[1])(functools.partial(take_face, 0, 1, field))
    pl.semaphore_wait(barrier, count)
    for k in range(2):
        pl.when(has[k])(face_copy(0, k).start)
    for k in range(2, 4):

        @pl.when(has[k])
        def _(k=k):
            build_face(k)
            take_face(0, k, field)
            face_copy(0, k).start()

    for k in range(4):
        pl.when(jnp.logical_not(has[k]))(functools.partial(build_face, k))

    def coarse_far(dy):
        return remote(
            c_all.at[g], c_all.at[g], cf_ssem.at[dy], c_rsem.at[g],
            a, z * ng + ((y + dy) % ny) * 2 + core,
        )

    def coarse_near(dy):
        which = ((y + dy) % ny) * 2 + core
        return remote(
            c_all.at[which], c_all.at[which], cp_ssem.at[dy], c_rsem.at[which], a, partner
        )

    def coarse_arrived(which):
        remote(
            c_all.at[which], c_all.at[which], cp_ssem.at[0], c_rsem.at[which], a, partner
        ).wait_recv()

    loads[1].wait()
    coarse_near(0).start()
    for dy in range(1, ny):
        coarse_far(dy).start()

    for step in range(STEPS):
        for k in range(4):

            @pl.when(jnp.logical_not(has[k]))
            def _(step=step, k=k):
                frecv[step, k * face : (k + 1) * face, :] = jnp.zeros((face, width), F32)

    def build_t(i, carry):
        at = rows_of(i, block)
        here = lax.broadcasted_iota(jnp.int32, (block, unknowns), 0) + i * block
        perm_t[at, :] = jnp.where(here.astype(F32) == rows_f, 1.0, 0.0).astype(BF16)
        return carry

    lax.fori_loop(0, blocks, build_t, 0)

    eye = lax.broadcasted_iota(jnp.int32, (prims, prims), 0) == lax.broadcasted_iota(
        jnp.int32, (prims, prims), 1
    )
    prim_row = prim_ref[...].astype(F32)
    prim_col = jnp.sum(jnp.where(eye, prim_row, 0.0), axis=1, keepdims=True)
    rate = jnp.sum(jnp.where(eye, decay_ref[...], 0.0), axis=1, keepdims=True)
    pick_t = jnp.where(
        prim_col == lax.broadcasted_iota(jnp.int32, (prims, unknowns), 1).astype(F32), 1.0, 0.0
    ).astype(BF16)
    pick = jnp.where(
        lax.broadcasted_iota(jnp.int32, (unknowns, prims), 0).astype(F32) == prim_row, 1.0, 0.0
    ).astype(BF16)

    def halves(source, high, low):
        def one(i, carry):
            at = rows_of(i, block)
            high[at, :], low[at, :] = split(source[at, :])
            return carry

        lax.fori_loop(0, blocks, one, 0)

    loads[2].wait()
    halves(n_buf, nh, nl)
    sel_h[...] = dot(pick_t, nh[...]).astype(BF16)
    sel_l[...] = dot(pick_t, nl[...]).astype(BF16)
    nph[...] = dot(sel_h[...], perm_t[...]).astype(BF16)
    npl[...] = dot(sel_l[...], perm_t[...]).astype(BF16)
    base[...] = dot3((sel_h[...], sel_l[...]), field)
    loads[3].wait()
    halves(d_buf, dh, dl)

    def pick_d(i, carry):
        at = rows_of(i, block)
        deh[at, :] = dot(dh[at, :], pick).astype(BF16)
        del_[at, :] = dot(dl[at, :], pick).astype(BF16)
        return carry

    lax.fori_loop(0, blocks, pick_d, 0)
    outs = [
        pltpu.make_async_copy(src, dst, out_sem.at[i])
        for i, (src, dst) in enumerate(
            [(deh, deh_hbm), (del_, del_hbm), (sol, t1_hbm), (res, t2_hbm)]
        )
    ]
    outs[0].start()
    outs[1].start()

    def pick_pd(i, carry):
        at = rows_of(i, block)
        pdeh[at, :] = dot(perm[at, :], deh[...]).astype(BF16)
        pdel[at, :] = dot(perm[at, :], del_[...]).astype(BF16)
        return carry

    lax.fori_loop(0, blocks, pick_pd, 0)

    order = [
        (dz, d)
        for dz in sorted(range(nz), key=lambda dz: -min(dz, nz - dz))
        for d in range(ng)
        if (dz, d) != (0, 0)
    ]

    def spread(step, dz, d):
        return remote(
            psend.at[step, mate_at[d]],
            gath.at[step, me],
            a_ssem.at[step, dz, d],
            g_rsem.at[step, me],
            a,
            ((z + dz) % nz) * ng + mate_at[d],
        )

    def arrived(step, who):
        remote(
            psend.at[step, 0], gath.at[step, who], a_ssem.at[step, 0, 0], g_rsem.at[step, who],
            a, partner,
        ).wait_recv()

    def q_copy(step, d):
        return remote(
            qsend.at[step, mate_at[d]], cown.at[step, g], q_ssem.at[step, d], q_rsem.at[step, g],
            a, mates[d],
        )

    def first_copy(step, d):
        return remote(
            qsend.at[step, mate_at[d]], cprev.at[step, g], p_ssem.at[step, d], p_rsem.at[step, g],
            a + 1, mates[d],
        )

    def next_copy(step, q):
        return remote(
            csend.at[step, q], cprev.at[step, q], p_ssem.at[step, q], p_rsem.at[step, q],
            a + 1, me,
        )

    starts = jnp.logical_and(a == 0, a < nx - 1)
    passes = jnp.logical_and(a > 0, a < nx - 1)

    for step in range(STEPS):
        last = step + 1 == STEPS
        source = r_buf if step == 0 else res
        for k in (2, 3, 0, 1):
            pl.when(has[k])(functools.partial(face_wait, step, k))
        ghost = split(frecv[step])
        prim = base[...] - dot3((nph[...], npl[...]), ghost)
        for q in range(ng):
            psend[step, q] = pack(prim[:, q * part : (q + 1) * part])
        for dz, d in order:
            spread(step, dz, d).start()
        gath[step, me] = psend[step, g]

        def fill(i, carry, source=source, ghost=ghost):
            at = rows_of(i, block)
            back = perm_t[at, :]
            jump[at, :] = source[at, :] - dot(back, ghost[0]) - dot(back, ghost[1])
            return carry

        lax.fori_loop(0, blocks, fill, 0)
        jumps = split(jump[...])

        def multiply(i, carry, jumps=jumps):
            at = rows_of(i, block)
            upd[at, :] = dot3((nh[at, :], nl[at, :]), jumps)
            return carry

        lax.fori_loop(0, blocks, multiply, 0)
        works = split(upd[...])
        if step == 0:
            for dy in range(1, ny):
                coarse_arrived(((y + dy) % ny) * 2 + core)
                coarse_near(dy).start()

        def smooth(i, carry, works=works, step=step):
            at = rows_of(i, block)
            update = dot3((dh[at, :], dl[at, :]), works)
            if step == 0:
                sol[at, :] = update
            else:
                sol[at, :] += update
            res[at, :] = jump[at, :] - 0.5 * update
            return carry

        lax.fori_loop(0, blocks // 2, smooth, 0)
        if step == 0:
            for dy in range(ny):
                coarse_arrived(((y + dy) % ny) * 2 + 1 - core)
        coarse = split(c_all[...].reshape(ng * prims, c_all.shape[2]))
        for dz, d in order:
            arrived(step, ((z + dz) % nz) * ng + mate_at[d])
        values = jnp.concatenate([unpack(gath[step, b]) for b in range(ny_all)], axis=0)
        quarter = dot3(coarse, split(values))
        for q in range(ng):
            qsend[step, q] = pack(quarter[q * prims : (q + 1) * prims, :])

        @pl.when(starts)
        def _(step=step):
            for d in range(ng):
                first_copy(step, d).start()

        for d in range(1, ng):
            q_copy(step, d).start()
        cown[step, g] = qsend[step, g]
        lax.fori_loop(blocks // 2, blocks, smooth, 0)
        if last:
            outs[2].start()
            outs[3].start()
        else:
            rests = split(res[...])
            for k in range(4):
                pl.when(has[k])(functools.partial(take_face, step + 1, k, rests))
        for d in range(1, ng):
            remote(
                qsend.at[step, 0], cown.at[step, mate_at[d]], q_ssem.at[step, 0],
                q_rsem.at[step, mate_at[d]], a, partner,
            ).wait_recv()

        def joined(ref, step=step):
            return jnp.concatenate([unpack(ref[step, q]) for q in range(ng)], axis=1)

        @pl.when(a == 0)
        def _(step=step):
            chain_ref[...] = joined(cown)

        @pl.when(a > 0)
        def _(step=step):
            for q in range(ng):
                next_copy(step, q).wait_recv()
            chain_ref[...] = joined(cown) + rate * joined(cprev)

        @pl.when(passes)
        def _(step=step):
            for q in range(ng):
                csend[step, q] = pack(chain_ref[:, q * part : (q + 1) * part])
                next_copy(step, q).start()

        if not last:
            chain = split(chain_ref[...])

            def late_face(k, step=step, chain=chain):
                at = pl.ds(k * face, face)
                fsend[step + 1, at, :] -= 0.5 * dot3((pdeh[at, :], pdel[at, :]), chain)
                face_copy(step + 1, k).start()

            for k in range(4):
                pl.when(has[k])(functools.partial(late_face, k))

            def finish(i, carry, chain=chain):
                at = rows_of(i, block)
                more = dot3((deh[at, :], del_[at, :]), chain)
                sol[at, :] += more
                res[at, :] -= 0.5 * more
                return carry

            lax.fori_loop(0, blocks, finish, 0)
            base[...] = dot3((sel_h[...], sel_l[...]), split(res[...]))

    for out in outs:
        out.wait()
    coarse_near(0).wait_send()
    for dy in range(1, ny):
        coarse_far(dy).wait_send()
        coarse_near(dy).wait_send()
    for step in range(STEPS):
        for k in range(4):
            pl.when(has[k])(face_copy(step, k).wait_send)
        for dz, d in order:
            spread(step, dz, d).wait_send()
        for d in range(1, ng):
            q_copy(step, d).wait_send()

        @pl.when(starts)
        def _(step=step):
            for d in range(ng):
                first_copy(step, d).wait_send()

        @pl.when(passes)
        def _(step=step):
            for q in range(ng):
                next_copy(step, q).wait_send()


def closing(t1, t2, deh, del_, chain, sol, res):
    more = dot3((deh[...], del_[...]), split(chain[...]))
    sol[...] = t1[...] + more
    res[...] = t2[...] - 0.5 * more


def local(nx, ny_all, residual_in, neumann, dirichlet, coarse, decay, face_rows, primal):
    unknowns, width = residual_in.shape[2:]
    prims = primal.shape[2]
    order = coarse.shape[2]
    nz, ny = line_sizes(ny_all)
    ng = 2 * ny
    part = width // ng
    fold = max(1, 128 // part)
    piece = (prims // fold, fold * part)
    anywhere = pl.BlockSpec(memory_space=pl.ANY)
    inside = pl.BlockSpec(memory_space=pltpu.VMEM)
    square = (unknowns, unknowns)
    field = (unknowns, width)
    slim = (unknowns, prims)
    dma = pltpu.SemaphoreType.DMA
    whole = jax.ShapeDtypeStruct(field, F32)
    thin = jax.ShapeDtypeStruct(slim, BF16)
    pieces = pl.pallas_call(
        functools.partial(kernel, nx, ny_all),
        out_shape=(whole, whole, thin, thin, jax.ShapeDtypeStruct((prims, width), F32)),
        in_specs=[anywhere] * 4 + [inside] * 3,
        out_specs=(anywhere, anywhere, anywhere, anywhere, inside),
        scratch_shapes=[
            pltpu.VMEM(square, F32),
            pltpu.VMEM(square, F32),
        ]
        + [pltpu.VMEM(square, BF16)] * 6
        + [pltpu.VMEM(field, F32)] * 5
        + [
            pltpu.VMEM((STEPS,) + field, F32),
            pltpu.VMEM((STEPS,) + field, F32),
            pltpu.VMEM((ng, prims, order), F32),
            pltpu.VMEM((STEPS, ng) + piece, F32),
            pltpu.VMEM((STEPS, ny_all) + piece, F32),
            pltpu.VMEM((STEPS, ng) + piece, F32),
            pltpu.VMEM((STEPS, ng) + piece, F32),
            pltpu.VMEM((STEPS, ng) + piece, F32),
            pltpu.VMEM((STEPS, ng) + piece, F32),
        ]
        + [pltpu.VMEM((prims, unknowns), BF16)] * 4
        + [pltpu.VMEM(slim, BF16)] * 4
        + [
            pltpu.VMEM((prims, width), F32),
            dma((4,)),
            dma((4,)),
            dma((ny,)),
            dma((ny,)),
            dma((ng,)),
            dma((STEPS, 4)),
            dma((STEPS, 4)),
            dma((STEPS, nz, ng)),
            dma((STEPS, ny_all)),
            dma((STEPS, ng)),
            dma((STEPS, ng)),
            dma((STEPS, ng)),
            dma((STEPS, ng)),
        ],
        compiler_params=pltpu.CompilerParams(
            collective_id=0, has_side_effects=True, vmem_limit_bytes=60000 * 1024
        ),
    )(
        residual_in[0, 0],
        neumann[0, 0],
        dirichlet[0, 0],
        coarse[0],
        decay[0],
        face_rows[0],
        primal[0],
    )
    rows = unknowns // 2
    tall = pl.BlockSpec((rows, width), lambda i: (i, 0))
    thin_block = pl.BlockSpec((rows, prims), lambda i: (i, 0))
    fixed = pl.BlockSpec((prims, width), lambda i: (0, 0))
    sol, res = pl.pallas_call(
        closing,
        grid=(2,),
        out_shape=(whole, whole),
        in_specs=[tall, tall, thin_block, thin_block, fixed],
        out_specs=(tall, tall),
    )(*pieces)
    return (sol[None, None], res[None, None])


def solution(mesh):
    return jax.shard_map(
        functools.partial(local, mesh.shape["gx"], mesh.shape["gy"]),
        mesh=mesh,
        in_specs=(
            P("gx", "gy", None, None),
            P("gx", "gy", None, None),
            P("gx", "gy", None, None),
            P("gx", "gy", None),
            P("gx", "gy", None),
            P("gx", "gy", None),
            P("gx", "gy", None),
        ),
        out_specs=(P("gx", "gy", None, None), P("gx", "gy", None, None)),
        check_vma=False,
    )
```
